128 devices in a mesh: side: 2 (over core), shard: 64 (over y, x, z).
Axes of the slice: x: 4, y: 4, z: 4, core: 2. Of those that a mesh axis runs over, the one named last changes fastest.
Arguments:
- sketch: bfloat16 [2, 131072, 128], P('side', 'shard'), may hold values from -6 to 6
- tile_values: bfloat16 [2, 327680, 1024], P('side', 'shard'), may hold values from -100 to 100, as said below
- sent_blocks: int32 [2, 2560], P(None, 'shard'), may hold values from 0 to 15, as said below
- pair_counts: int32 [2, 320], P(None, 'shard'), may hold values from 4 to 8, as said below
Outputs:
- new_sketch: float32 [2, 131072, 128], P('side', 'shard')
The draws below stay inside these ranges and needn't reach their ends.
Inputs may be any that keep to these rules, and one draw needn't show every extreme that they name: The two sides hold one matrix: tile_values[1, o, j] is the transpose of tile_values[0, (o + j - 2) mod 64, 4 - j] in the layout of the first step. `sent_blocks`: the 8 entries of one side, owner and pair are distinct. `pair_counts`: for every side and owner some pair uses all 8 slots.
All inputs are finite; a program needn't handle non-finite values.
Results may differ from the reference program's by a relative error of at most 0.0003.
Values may be sent and summed in bfloat16 or wider, within the bound.
A program may use at most 64 MiB of HBM per device.

```python
import math
import jax
import jax.numpy as jnp
from jax import lax

TB = 128
RANK = 128
BLK_DEV = 16
PEER = 8
HALF = 2
PAIRS = 5
OWNERS = 64
ROWS = 131072


def tile_pattern(key, flat_pair):
    extent = PEER * TB
    source = jax.random.fold_in(key, flat_pair)
    normal_key, row_key, column_key = jax.random.split(source, 3)
    values = jnp.clip(jax.random.normal(normal_key, (extent, extent), jnp.float32), -6.0, 6.0)
    spread = math.log(10.0)
    growth = 0.5 * math.log(3.0)
    row_scale = jnp.exp(jax.random.uniform(row_key, (extent,), jnp.float32, 0.0, spread))
    column_scale = jnp.exp(jax.random.uniform(column_key, (extent,), jnp.float32, 0.0, spread))
    owner_pos = (flat_pair // PAIRS).astype(jnp.float32)
    trend = jnp.exp(growth * owner_pos / max(OWNERS - 1, 1))
    scaled = values * row_scale[:, None] * column_scale[None, :] * trend / math.sqrt(PAIRS * PEER * TB)
    return jnp.clip(scaled, -100.0, 100.0)


def draw_tile_values(key, part):
    extent = PEER * TB
    count_pairs = OWNERS * PAIRS

    def user_side(flat_pair):
        return tile_pattern(key, flat_pair).astype(jnp.bfloat16)

    def item_side(flat_pair):
        owner_pos = flat_pair // PAIRS
        pair_pos = flat_pair % PAIRS
        partner = (owner_pos + pair_pos - HALF) % OWNERS
        return tile_pattern(key, partner * PAIRS + (PAIRS - 1 - pair_pos)).T.astype(jnp.bfloat16)
    flats = jnp.arange(count_pairs, dtype=jnp.int32)
    first = lax.map(user_side, flats)
    second = lax.map(item_side, flats)
    return jnp.stack([first, second]).reshape(2, count_pairs * extent, extent)


def draw_sent_blocks(key, part):
    own_key = jax.random.fold_in(key, 11)
    rows_total = 2 * OWNERS * PAIRS
    scores = jax.random.randint(own_key, (rows_total, BLK_DEV), 0, 2 ** 20, dtype=jnp.int32)
    scores = scores * BLK_DEV + jnp.arange(BLK_DEV, dtype=jnp.int32)[None, :]
    chosen = jnp.argsort(scores, axis=1)[:, :PEER]
    return chosen.astype(jnp.int32).reshape(2, OWNERS * PAIRS * PEER)


def draw_pair_counts(key, part):
    own_key = jax.random.fold_in(key, 23)
    count_key, full_key = jax.random.split(own_key, 2)
    counts = jax.random.randint(count_key, (2, OWNERS, PAIRS), PEER // 2, PEER + 1, dtype=jnp.int32)
    full_pair = jax.random.randint(full_key, (2, OWNERS, 1), 0, PAIRS, dtype=jnp.int32)
    places = jnp.arange(PAIRS, dtype=jnp.int32)[None, None, :]
    counts = jnp.where(places == full_pair, PEER, counts)
    return counts.astype(jnp.int32).reshape(2, OWNERS * PAIRS)


def levels(rng, dims, pieces, smallest, high):
    level = 1.0
    for position, parts in pieces:
        steps = jax.random.uniform(jax.random.fold_in(jax.random.fold_in(rng, 6), position), (parts,), jnp.float32, smallest / len(pieces), high / len(pieces))
        level = level * jnp.repeat(jnp.exp(steps), dims[position] // parts).reshape((-1,) + (1,) * (len(dims) - 1 - position))
    return level


def gaussian(key, shape, scale, reach, pieces=(), kind=jnp.bfloat16):
    result = scale * jax.random.normal(key, shape, jnp.float32)
    if pieces:
        result = result * levels(key, shape, pieces, -0.22, 0.18)
    return jnp.clip(result, -reach, reach).astype(kind)


def setup_inputs(seed: int = 0) -> dict:
    seeds = jax.random.split(jax.random.key(seed), 5)
    sketch = gaussian(seeds[0], (2, ROWS, RANK), 1.0, 6.0, ((0, 2), (1, 64)))
    tile_values = draw_tile_values(jax.random.fold_in(seeds[4], 71), 0)
    sent_blocks = draw_sent_blocks(jax.random.fold_in(seeds[4], 71), 0)
    pair_counts = draw_pair_counts(jax.random.fold_in(seeds[4], 71), 0)
    return dict(sketch=sketch, tile_values=tile_values, sent_blocks=sent_blocks, pair_counts=pair_counts)


EPSILON = 1e-05

def side_update(own_side, sketch, tile_values, sent_blocks, pair_counts):
    far_side = 1 - own_side
    block_lists = sent_blocks.reshape(2, OWNERS, PAIRS, PEER)
    block_counts = pair_counts.reshape(2, OWNERS, PAIRS)
    far_sketch = sketch[far_side].reshape(OWNERS, BLK_DEV, TB, RANK)
    tile_grid = tile_values[own_side].reshape(OWNERS, PAIRS, PEER * TB, PEER * TB)
    offsets = jnp.arange(PAIRS, dtype=jnp.int32) - HALF
    mirror = (PAIRS - 1 - jnp.arange(PAIRS, dtype=jnp.int32)).astype(jnp.int32)
    places = jnp.arange(PEER, dtype=jnp.int32)
    targets = jnp.arange(BLK_DEV, dtype=jnp.int32)

    def one_owner(owner_pos):
        partner = ((owner_pos + offsets) % OWNERS).astype(jnp.int32)
        far_lists = block_lists[far_side][partner, mirror]
        far_counts = block_counts[far_side][partner, mirror]
        fetched = far_sketch[partner[:, None], far_lists]
        usable_far = places[None, :] < far_counts[:, None]
        fetched = jnp.where(usable_far[:, :, None, None], fetched, jnp.zeros_like(fetched))
        fetched = fetched.reshape(PAIRS, PEER * TB, RANK).astype(jnp.float32)
        product = jnp.einsum('jab,jbr->jar', tile_grid[owner_pos].astype(jnp.float32), fetched, precision=lax.Precision.HIGHEST)
        own_lists = block_lists[own_side][owner_pos]
        own_counts = block_counts[own_side][owner_pos]
        usable_own = places[None, :] < own_counts[:, None]
        routing = ((own_lists[:, :, None] == targets[None, None, :]) & usable_own[:, :, None]).astype(jnp.float32)
        return jnp.einsum('jak,jatr->ktr', routing, product.reshape(PAIRS, PEER, TB, RANK), precision=lax.Precision.HIGHEST)
    update = lax.map(one_owner, jnp.arange(OWNERS, dtype=jnp.int32)).reshape(ROWS, RANK)
    gram_matrix = jnp.dot(update.T, update, precision=lax.Precision.HIGHEST) / ROWS
    gram_matrix = gram_matrix + EPSILON * jnp.eye(RANK, dtype=jnp.float32)
    factor = jnp.linalg.cholesky(gram_matrix)
    return jax.scipy.linalg.solve_triangular(factor, update.T, lower=True).T

def reference(sketch, tile_values, sent_blocks, pair_counts):
    users_new = side_update(0, sketch, tile_values, sent_blocks, pair_counts)
    items_new = side_update(1, sketch, tile_values, sent_blocks, pair_counts)
    return jnp.stack([users_new, items_new])
```

```python
import functools

import jax
import jax.numpy as jnp
from jax import lax
from jax.experimental import pallas as pl
from jax.experimental.pallas import tpu as pltpu
from jax.sharding import PartitionSpec as P

TB = 128
RANK = 128
PEER = 8
HALF = 2
PAIRS = 5
BLOCKS = 16
EDGE = PEER * TB
CHUNKS = 4
CROWS = EDGE // CHUNKS
PLANE = 16
EPSILON = 1e-05
F32 = jnp.float32
BF16 = jnp.bfloat16
MESH = pl.DeviceIdType.MESH
HIGHEST = lax.Precision.HIGHEST


def exchange_kernel(
    owners,
    lists_hbm,
    counts_hbm,
    sk_hbm,
    tile_hbm,
    u_hbm,
    gsum,
    lists,
    counts,
    sk,
    tile,
    send,
    recv,
    relay,
    prod,
    u,
    inv,
    gpart,
    rs,
    ybuf,
    in_sem,
    tile_sem,
    a_send,
    a_recv,
    r_send,
    r_recv,
    b_send,
    b_recv,
    rs_send,
    rs_recv,
    y_send,
    y_recv,
    ag_send,
    ag_recv,
):
    side = lax.axis_index("side")
    me = lax.axis_index("shard")
    far = 1 - side
    ahead = lax.rem(me + 1, owners)
    behind = lax.rem(me + owners - 1, owners)
    planes = owners // PLANE
    q = lax.rem(me, PLANE)
    y = me // PLANE
    base = y * PLANE

    inputs = []
    for n, (src, dst) in enumerate(((sk_hbm, sk), (lists_hbm, lists), (counts_hbm, counts))):
        c = pltpu.make_async_copy(src, dst, in_sem.at[n])
        c.start()
        inputs.append(c)
    tile_copies = {}
    for j in (2, 1, 3, 0, 4):
        c = pltpu.make_async_copy(tile_hbm.at[j], tile.at[j], tile_sem.at[j])
        c.start()
        tile_copies[j] = c

    barrier = pltpu.get_barrier_semaphore()
    greet = [(far, ahead), (far, behind), (far, me), (side, ahead), (side, behind)]
    greet += [(side, base + lax.rem(q + i, PLANE)) for i in range(1, PLANE)]
    greet += [(side, lax.rem(me + i * PLANE, owners)) for i in range(1, planes)]
    for d in greet:
        pl.semaphore_signal(barrier, inc=1, device_id=d, device_id_type=MESH)

    for c in inputs:
        c.wait()
    for j in (4, 0, 3, 1, 2):
        live = counts[side, j]

        def pack(b, carry, j=j, live=live):
            block = sk[lists[side, j * PEER + b]]
            keep = jnp.where(b < live, 1.0, 0.0).astype(BF16)
            send[j, pl.ds(pl.multiple_of(b * TB, TB), TB), :] = block * keep
            return carry

        lax.fori_loop(0, PEER, pack, 0)

    pl.semaphore_wait(barrier, len(greet))

    def remote(src, dst, ss, rsem, dev):
        c = pltpu.make_async_remote_copy(
            src_ref=src, dst_ref=dst, send_sem=ss, recv_sem=rsem, device_id=dev, device_id_type=MESH
        )
        return c

    rows = [pl.ds(i * CROWS, CROWS) for i in range(CHUNKS)]
    a_copies = [[], []]
    for i in range(CHUNKS):
        for way, (jj, to) in enumerate(((4, ahead), (0, behind))):
            c = remote(
                send.at[jj, rows[i]], relay.at[way, rows[i]], a_send.at[way, i], a_recv.at[way, i], (far, to)
            )
            c.start()
            a_copies[way].append(c)
    b_copies = {}
    for jj, to in ((2, me), (3, ahead), (1, behind)):
        c = remote(send.at[jj], recv.at[4 - jj], b_send.at[jj], b_recv.at[4 - jj], (far, to))
        c.start()
        b_copies[4 - jj] = c

    def table(n, carry):
        j = n // BLOCKS
        k = lax.rem(n, BLOCKS)
        place = jnp.int32(PEER)
        live = counts[side, j]
        for a in range(PEER):
            hit = jnp.logical_and(lists[side, j * PEER + a] == k, a < live)
            place = jnp.where(hit, jnp.int32(a), place)
        inv[n] = place
        return carry

    lax.fori_loop(0, PAIRS * BLOCKS, table, 0)
    for j in range(PAIRS):
        prod[j, PEER] = jnp.zeros((TB, RANK), F32)

    def multiply(j, k0, depth, first):
        def step(a, carry):
            at = pl.ds(pl.multiple_of(a * 2 * TB, 2 * TB), 2 * TB)
            part = jnp.dot(
                tile[j, at, k0 : k0 + depth], recv[j, k0 : k0 + depth, :], preferred_element_type=F32
            ).reshape(2, TB, RANK)
            where = pl.ds(a * 2, 2)
            if first:
                prod[j, where] = part
            else:
                prod[j, where] = prod[j, where] + part
            return carry

        lax.fori_loop(0, PEER // 2, step, 0)

    b_copies[2].wait_recv()
    tile_copies[2].wait()
    multiply(2, 0, EDGE, True)

    r_copies = [[], []]
    for i in range(CHUNKS):
        for way, (j, to) in enumerate(((0, ahead), (4, behind))):
            a_copies[way][i].wait_recv()
            c = remote(
                relay.at[way, rows[i]], recv.at[j, rows[i]], r_send.at[way, i], r_recv.at[way, i], (side, to)
            )
            c.start()
            r_copies[way].append(c)

    for j in (1, 3):
        b_copies[j].wait_recv()
        tile_copies[j].wait()
        multiply(j, 0, EDGE, True)

    def gather_near(k, carry):
        u[k] = (
            prod[1, inv[BLOCKS + k]] + prod[2, inv[2 * BLOCKS + k]] + prod[3, inv[3 * BLOCKS + k]]
        )
        return carry

    lax.fori_loop(0, BLOCKS, gather_near, 0)

    tile_copies[0].wait()
    tile_copies[4].wait()
    for i in range(CHUNKS):
        for way, j in enumerate((0, 4)):
            r_copies[way][i].wait_recv()
            multiply(j, i * CROWS, CROWS, i == 0)

    gpart[...] = jnp.zeros((RANK, RANK), F32)

    def gather_far(k, carry):
        block = u[k] + prod[0, inv[k]] + prod[4, inv[4 * BLOCKS + k]]
        u[k] = block
        gpart[...] += lax.dot_general(
            block, block, (((0,), (0,)), ((), ())), precision=HIGHEST, preferred_element_type=F32
        )
        return carry

    lax.fori_loop(0, BLOCKS, gather_far, 0)
    u_copy = pltpu.make_async_copy(u, u_hbm, in_sem.at[3])
    u_copy.start()
    rs_copies = []
    for i in range(1, PLANE):
        to = lax.rem(q + i, PLANE)
        c = remote(
            gpart.at[pl.ds(pl.multiple_of(to * 8, 8), 8)],
            rs.at[i],
            rs_send.at[i],
            rs_recv.at[i],
            (side, base + to),
        )
        c.start()
        rs_copies.append(c)
    total = gpart[pl.ds(pl.multiple_of(q * 8, 8), 8), :]
    for i in range(1, PLANE):
        rs_copies[i - 1].wait_recv()
        total = total + rs[i]
    ybuf[0] = total
    y_copies = []
    for i in range(1, planes):
        c = remote(
            ybuf.at[0], ybuf.at[i], y_send.at[i], y_recv.at[i], (side, lax.rem(me + i * PLANE, owners))
        )
        c.start()
        y_copies.append(c)
    for c in y_copies:
        c.wait_recv()
    total = ybuf[0]
    for i in range(1, planes):
        total = total + ybuf[i]
    mine = pl.ds(pl.multiple_of(q * 8, 8), 8)
    gsum[mine, :] = total
    ag_copies = []
    for i in range(1, PLANE):
        to = lax.rem(q + i, PLANE)
        c = remote(gsum.at[mine], gsum.at[mine], ag_send.at[i], ag_recv.at[i], (side, base + to))
        c.start()
        ag_copies.append(c)
    for i in range(1, PLANE):
        src = pl.ds(pl.multiple_of(lax.rem(q + PLANE - i, PLANE) * 8, 8), 8)
        remote(gsum.at[src], gsum.at[src], ag_send.at[i], ag_recv.at[i], (side, me)).wait_recv()

    for group in (a_copies[0], a_copies[1], r_copies[0], r_copies[1], rs_copies, y_copies, ag_copies):
        for c in group:
            c.wait_send()
    for c in b_copies.values():
        c.wait_send()
    u_copy.wait()


def exchange(owners, lists, counts, sketch, tiles):
    dma = pltpu.SemaphoreType.DMA
    vmem = pl.BlockSpec(memory_space=pltpu.VMEM)
    hbm = pl.BlockSpec(memory_space=pl.ANY)
    planes = owners // PLANE
    return pl.pallas_call(
        functools.partial(exchange_kernel, owners),
        name="exchange",
        out_shape=(
            jax.ShapeDtypeStruct((BLOCKS, TB, RANK), F32),
            jax.ShapeDtypeStruct((RANK, RANK), F32),
        ),
        in_specs=[hbm, hbm, hbm, hbm],
        out_specs=(hbm, vmem),
        scratch_shapes=[
            pltpu.SMEM((2, PAIRS * PEER), jnp.int32),
            pltpu.SMEM((2, PAIRS), jnp.int32),
            pltpu.VMEM((BLOCKS, TB, RANK), BF16),
            pltpu.VMEM((PAIRS, EDGE, EDGE), BF16),
            pltpu.VMEM((PAIRS, EDGE, RANK), BF16),
            pltpu.VMEM((PAIRS, EDGE, RANK), BF16),
            pltpu.VMEM((2, EDGE, RANK), BF16),
            pltpu.VMEM((PAIRS, PEER + 1, TB, RANK), F32),
            pltpu.VMEM((BLOCKS, TB, RANK), F32),
            pltpu.SMEM((PAIRS * BLOCKS,), jnp.int32),
            pltpu.VMEM((RANK, RANK), F32),
            pltpu.VMEM((PLANE, 8, RANK), F32),
            pltpu.VMEM((planes, 8, RANK), F32),
            dma((4,)),
            dma((PAIRS,)),
            dma((2, CHUNKS)),
            dma((2, CHUNKS)),
            dma((2, CHUNKS)),
            dma((2, CHUNKS)),
            dma((PAIRS,)),
            dma((PAIRS,)),
            dma((PLANE,)),
            dma((PLANE,)),
            dma((planes,)),
            dma((planes,)),
            dma((PLANE,)),
            dma((PLANE,)),
        ],
        compiler_params=pltpu.CompilerParams(
            collective_id=0, has_side_effects=True, vmem_limit_bytes=67043328
        ),
    )(lists, counts, sketch, tiles)


STEPS = 4


def finish_kernel(rows, g, u_hbm, out_hbm, u, o, am, u_sem, o_sem):
    u_copy = pltpu.make_async_copy(u_hbm, u, u_sem)
    u_copy.start()
    row = lax.broadcasted_iota(jnp.int32, (RANK, RANK), 0)
    col = lax.broadcasted_iota(jnp.int32, (RANK, RANK), 1)
    eye = jnp.where(row == col, 1.0, 0.0).astype(F32)
    am[0] = g[...] * (1.0 / rows) + EPSILON * eye
    am[1] = eye
    sub = lax.broadcasted_iota(jnp.int32, (8, RANK), 0)
    for p in range(RANK // 8):
        lo = 8 * p
        blocks = RANK // 8 - p
        a = [am[0, lo + 8 * t : lo + 8 * t + 8, :] for t in range(blocks)]
        m = [am[1, lo + 8 * t : lo + 8 * t + 8, :] for t in range(blocks)]
        c = [
            [jnp.broadcast_to(a[t][:, lo + j : lo + j + 1], (8, RANK)) for t in range(blocks)]
            for j in range(8)
        ]
        diag = None
        for k in range(8):
            pivot = jnp.broadcast_to(c[k][0][k : k + 1, :], (8, RANK))
            diag = pivot if diag is None else jnp.where(sub == k, pivot, diag)
            recip = 1.0 / pivot
            mult = [c[k][t] * recip for t in range(blocks)]
            mult[0] = jnp.where(sub > k, mult[0], 0.0)
            for j in range(k + 1, 8):
                f = jnp.broadcast_to(c[j][0][k : k + 1, :], (8, RANK))
                for t in range(blocks):
                    c[j][t] = c[j][t] - mult[t] * f
            arow = jnp.broadcast_to(a[0][k : k + 1, :], (8, RANK))
            mrow = jnp.broadcast_to(m[0][k : k + 1, :], (8, RANK))
            for t in range(blocks):
                a[t] = a[t] - mult[t] * arow
                m[t] = m[t] - mult[t] * mrow
        am[1, lo : lo + 8, :] = m[0] * lax.rsqrt(diag)
        for t in range(1, blocks):
            am[0, lo + 8 * t : lo + 8 * t + 8, :] = a[t]
            am[1, lo + 8 * t : lo + 8 * t + 8, :] = m[t]
    u_copy.wait()
    w = am[1]
    step = (BLOCKS * TB) // STEPS
    copies = []
    for s in range(STEPS):
        at = pl.ds(s * step, step)
        o[at, :] = lax.dot_general(
            u[at, :], w, (((1,), (1,)), ((), ())), precision=HIGHEST, preferred_element_type=F32
        )
        c = pltpu.make_async_copy(o.at[at], out_hbm.at[at], o_sem.at[s])
        c.start()
        copies.append(c)
    for c in copies:
        c.wait()


def finish(rows, g, u):
    n = BLOCKS * TB
    return pl.pallas_call(
        functools.partial(finish_kernel, rows),
        name="finish",
        out_shape=jax.ShapeDtypeStruct((n, RANK), F32),
        in_specs=[pl.BlockSpec(memory_space=pltpu.VMEM), pl.BlockSpec(memory_space=pl.ANY)],
        out_specs=pl.BlockSpec(memory_space=pl.ANY),
        scratch_shapes=[
            pltpu.VMEM((n, RANK), F32),
            pltpu.VMEM((n, RANK), F32),
            pltpu.VMEM((2, RANK, RANK), F32),
            pltpu.SemaphoreType.DMA(()),
            pltpu.SemaphoreType.DMA((STEPS,)),
        ],
        compiler_params=pltpu.CompilerParams(vmem_limit_bytes=67043328),
    )(g, u)


def body(sketch, tile_values, sent_blocks, pair_counts):
    owners = lax.axis_size("shard")
    tiles = tile_values[0].reshape(PAIRS, EDGE, EDGE)
    u, g = exchange(owners, sent_blocks, pair_counts, sketch[0].reshape(BLOCKS, TB, RANK), tiles)
    rows = BLOCKS * TB * owners
    return finish(rows, g, u.reshape(BLOCKS * TB, RANK))[None]


def solution(mesh):
    return jax.shard_map(
        body,
        mesh=mesh,
        in_specs=(
            P("side", "shard", None),
            P("side", "shard", None),
            P(None, "shard"),
            P(None, "shard"),
        ),
        out_specs=P("side", "shard", None),
        check_vma=False,
    )
```

```python
import functools

import jax
import jax.numpy as jnp
from jax import lax
from jax.experimental import pallas as pl
from jax.experimental.pallas import tpu as pltpu
from jax.sharding import PartitionSpec as P

TB = 128
RANK = 128
PEER = 8
HALF = 2
PAIRS = 5
BLOCKS = 16
EDGE = PEER * TB
CHUNKS = 4
CROWS = EDGE // CHUNKS
RING = 4
PLANE = 16
EPSILON = 1e-05
F32 = jnp.float32
BF16 = jnp.bfloat16
MESH = pl.DeviceIdType.MESH
HIGHEST = lax.Precision.HIGHEST


def split(x):
    high = x.astype(BF16)
    rest = x - high.astype(F32)
    middle = rest.astype(BF16)
    return high, middle, (rest - middle.astype(F32)).astype(BF16)


def gram(x):
    def cross(a, b):
        return lax.dot_general(a, b, (((0,), (0,)), ((), ())), preferred_element_type=F32)

    high, middle, low = split(x)
    pair = jnp.concatenate([high, middle], 1)
    both = cross(pair, pair)
    mixed = both[:RANK, RANK:] + cross(high, low)
    return both[:RANK, :RANK] + both[RANK:, RANK:] + mixed + mixed.T


def exchange_kernel(
    owners,
    lists_hbm,
    counts_hbm,
    sk_hbm,
    tile_hbm,
    u_parts,
    gsum,
    lists,
    counts,
    sk,
    tile,
    send,
    recv,
    relay,
    prod,
    u,
    inv,
    gpart,
    rs,
    ybuf,
    in_sem,
    tile_sem,
    a_send,
    a_recv,
    r_send,
    r_recv,
    b_send,
    b_recv,
    rs_send,
    rs_recv,
    y_send,
    y_recv,
    ag_send,
    ag_recv,
    plane_sem,
    hello_sem,
):
    side = lax.axis_index("side")
    me = lax.axis_index("shard")
    far = 1 - side
    ahead = lax.rem(me + 1, owners)
    behind = lax.rem(me + owners - 1, owners)
    planes = owners // PLANE
    q = lax.rem(me, PLANE)
    y = me // PLANE
    base = y * PLANE

    inputs = []
    for n, (src, dst) in enumerate(((sk_hbm, sk), (lists_hbm, lists), (counts_hbm, counts))):
        c = pltpu.make_async_copy(src, dst, in_sem.at[n])
        c.start()
        inputs.append(c)
    def signal(sem, device):
        pl.semaphore_signal(sem, inc=1, device_id=device, device_id_type=MESH)

    ring_z = [(side, me - lax.rem(me, RING) + lax.rem(me + i, RING)) for i in range(1, RING)]
    ring_x = [(side, base + lax.rem(q + i * RING, PLANE)) for i in range(1, RING)]
    ring_y = [(side, lax.rem(me + i * PLANE, owners)) for i in range(1, planes)]
    across = [(far, ahead), (far, behind), (far, me)]
    greet = [(side, ahead), (side, behind)] + ring_z + ring_x + ring_y
    barrier = pltpu.get_barrier_semaphore()
    for device in greet:
        signal(barrier, device)

    @pl.when(side == 0)
    def _():
        for device in across:
            signal(barrier, device)

    for c in inputs:
        c.wait()

    def pack(j):
        live = counts[side, j]
        for b in range(PEER):
            keep = jnp.where(b < live, 1.0, 0.0).astype(BF16)
            send[j, b * TB : (b + 1) * TB, :] = sk[lists[side, j * PEER + b]] * keep

    for j in (4, 0):
        pack(j)

    pl.semaphore_wait(barrier, len(greet) + side * len(across))
    for device in ring_x:
        signal(plane_sem, device)

    @pl.when(side == 1)
    def _():
        for device in across:
            signal(hello_sem, device)

    def remote(src, dst, ss, rsem, dev):
        c = pltpu.make_async_remote_copy(
            src_ref=src, dst_ref=dst, send_sem=ss, recv_sem=rsem, device_id=dev, device_id_type=MESH
        )
        return c

    rows = [pl.ds(i * CROWS, CROWS) for i in range(CHUNKS)]
    a_copies = [[], []]
    for i in range(CHUNKS):
        for way, (jj, to) in enumerate(((4, ahead), (0, behind))):
            c = remote(
                send.at[jj, rows[i]], relay.at[way, rows[i]], a_send.at[way, i], a_recv.at[way, i], (side, to)
            )
            c.start()
            a_copies[way].append(c)
    for j in (3, 1, 2):
        pack(j)

    @pl.when(side == 0)
    def _():
        pl.semaphore_wait(hello_sem, len(across))

    b_copies = {}
    for jj, to in ((2, me), (3, ahead), (1, behind)):
        c = remote(send.at[jj], recv.at[4 - jj], b_send.at[jj], b_recv.at[4 - jj], (far, to))
        c.start()
        b_copies[4 - jj] = c

    tile_copies = {}
    for j in (2, 1, 3, 0, 4):
        c = pltpu.make_async_copy(tile_hbm.at[j], tile.at[j], tile_sem.at[j])
        c.start()
        tile_copies[j] = c

    def table(n, carry):
        j = n // BLOCKS
        k = lax.rem(n, BLOCKS)
        place = jnp.int32(PEER)
        live = counts[side, j]
        for a in range(PEER):
            hit = jnp.logical_and(lists[side, j * PEER + a] == k, a < live)
            place = jnp.where(hit, jnp.int32(a), place)
        inv[n] = place
        return carry

    lax.fori_loop(0, PAIRS * BLOCKS, table, 0)
    for j in range(PAIRS):
        prod[j, PEER] = jnp.zeros((TB, RANK), F32)

    def multiply(j, k0, depth, first):
        def step(a, carry):
            at = pl.ds(pl.multiple_of(a * 2 * TB, 2 * TB), 2 * TB)
            part = jnp.dot(
                tile[j, at, k0 : k0 + depth], recv[j, k0 : k0 + depth, :], preferred_element_type=F32
            ).reshape(2, TB, RANK)
            where = pl.ds(a * 2, 2)
            if first:
                prod[j, where] = part
            else:
                prod[j, where] = prod[j, where] + part
            return carry

        lax.fori_loop(0, PEER // 2, step, 0)

    b_copies[2].wait_recv()
    tile_copies[2].wait()
    multiply(2, 0, EDGE, True)

    r_copies = [[], []]
    for i in range(CHUNKS):
        for way, (j, to) in enumerate(((0, ahead), (4, behind))):
            a_copies[way][i].wait_recv()
            c = remote(
                relay.at[way, rows[i]], recv.at[j, rows[i]], r_send.at[way, i], r_recv.at[way, i], (far, to)
            )
            c.start()
            r_copies[way].append(c)

    for j in (1, 3):
        b_copies[j].wait_recv()
        tile_copies[j].wait()
        multiply(j, 0, EDGE, True)

    def gather_near(k, carry):
        u[k] = (
            prod[1, inv[BLOCKS + k]] + prod[2, inv[2 * BLOCKS + k]] + prod[3, inv[3 * BLOCKS + k]]
        )
        return carry

    lax.fori_loop(0, BLOCKS, gather_near, 0)

    tile_copies[0].wait()
    tile_copies[4].wait()
    for i in range(CHUNKS):
        for way, j in enumerate((0, 4)):
            r_copies[way][i].wait_recv()
            part = jnp.dot(
                tile[j, :, i * CROWS : (i + 1) * CROWS], recv[j, rows[i], :], preferred_element_type=F32
            ).reshape(PEER, TB, RANK)
            if i == 0:
                prod[j, 0:PEER] = part
            else:
                prod[j, 0:PEER] = prod[j, 0:PEER] + part

    for k in range(BLOCKS):
        u[k] = u[k] + prod[0, inv[k]] + prod[4, inv[4 * BLOCKS + k]]
    gpart[...] = gram(u[...].reshape(BLOCKS * TB, RANK))

    pl.semaphore_wait(plane_sem, len(ring_x))
    rs_copies = []
    for i in range(1, PLANE):
        to = lax.rem(q + i, PLANE)
        c = remote(
            gpart.at[pl.ds(pl.multiple_of(to * 8, 8), 8)],
            rs.at[i],
            rs_send.at[i],
            rs_recv.at[i],
            (side, base + to),
        )
        c.start()
        rs_copies.append(c)
    def part(k, carry):
        at = pl.ds(pl.multiple_of(k * TB, TB), TB)
        for n, piece in enumerate(split(u[k])):
            u_parts[at, n * RANK : (n + 1) * RANK] = piece
        return carry

    lax.fori_loop(0, BLOCKS, part, 0)
    total = gpart[pl.ds(pl.multiple_of(q * 8, 8), 8), :]
    for i in range(1, PLANE):
        rs_copies[i - 1].wait_recv()
        total = total + rs[i]
    ybuf[0] = total
    y_copies = []
    for i in range(1, planes):
        c = remote(
            ybuf.at[0], ybuf.at[i], y_send.at[i], y_recv.at[i], (side, lax.rem(me + i * PLANE, owners))
        )
        c.start()
        y_copies.append(c)
    for c in y_copies:
        c.wait_recv()
    total = ybuf[0]
    for i in range(1, planes):
        total = total + ybuf[i]
    mine = pl.ds(pl.multiple_of(q * 8, 8), 8)
    gsum[mine, :] = total
    ag_copies = []
    for i in range(1, PLANE):
        to = lax.rem(q + i, PLANE)
        c = remote(gsum.at[mine], gsum.at[mine], ag_send.at[i], ag_recv.at[i], (side, base + to))
        c.start()
        ag_copies.append(c)
    for i in range(1, PLANE):
        src = pl.ds(pl.multiple_of(lax.rem(q + PLANE - i, PLANE) * 8, 8), 8)
        remote(gsum.at[src], gsum.at[src], ag_send.at[i], ag_recv.at[i], (side, me)).wait_recv()

    for group in (a_copies[0], a_copies[1], r_copies[0], r_copies[1], rs_copies, y_copies, ag_copies):
        for c in group:
            c.wait_send()
    for c in b_copies.values():
        c.wait_send()


def exchange(owners, lists, counts, sketch, tiles):
    dma = pltpu.SemaphoreType.DMA
    vmem = pl.BlockSpec(memory_space=pltpu.VMEM)
    hbm = pl.BlockSpec(memory_space=pl.ANY)
    planes = owners // PLANE
    return pl.pallas_call(
        functools.partial(exchange_kernel, owners),
        name="exchange",
        out_shape=(
            pltpu.VMEM((BLOCKS * TB, 3 * RANK), BF16),
            pltpu.VMEM((RANK, RANK), F32),
        ),
        in_specs=[hbm, hbm, hbm, hbm],
        out_specs=(vmem, vmem),
        scratch_shapes=[
            pltpu.SMEM((2, PAIRS * PEER), jnp.int32),
            pltpu.SMEM((2, PAIRS), jnp.int32),
            pltpu.VMEM((BLOCKS, TB, RANK), BF16),
            pltpu.VMEM((PAIRS, EDGE, EDGE), BF16),
            pltpu.VMEM((PAIRS, EDGE, RANK), BF16),
            pltpu.VMEM((PAIRS, EDGE, RANK), BF16),
            pltpu.VMEM((2, EDGE, RANK), BF16),
            pltpu.VMEM((PAIRS, PEER + 1, TB, RANK), F32),
            pltpu.VMEM((BLOCKS, TB, RANK), F32),
            pltpu.SMEM((PAIRS * BLOCKS,), jnp.int32),
            pltpu.VMEM((RANK, RANK), F32),
            pltpu.VMEM((PLANE, 8, RANK), F32),
            pltpu.VMEM((planes, 8, RANK), F32),
            dma((3,)),
            dma((PAIRS,)),
            dma((2, CHUNKS)),
            dma((2, CHUNKS)),
            dma((2, CHUNKS)),
            dma((2, CHUNKS)),
            dma((PAIRS,)),
            dma((PAIRS,)),
            dma((PLANE,)),
            dma((PLANE,)),
            dma((planes,)),
            dma((planes,)),
            dma((PLANE,)),
            dma((PLANE,)),
            pltpu.SemaphoreType.REGULAR,
            pltpu.SemaphoreType.REGULAR,
        ],
        compiler_params=pltpu.CompilerParams(
            collective_id=0, has_side_effects=True, vmem_limit_bytes=40 * 1024 * 1024
        ),
    )(*[pltpu.with_memory_space_constraint(x, pltpu.HBM) for x in (lists, counts, sketch, tiles)])


STEPS = 4


def along(a, b):
    return lax.dot_general(a, b, (((1,), (1,)), ((), ())), preferred_element_type=F32)


def finish_kernel(rows, g, u, out_hbm, o, am, o_sem):
    row = lax.broadcasted_iota(jnp.int32, (RANK, RANK), 0)
    col = lax.broadcasted_iota(jnp.int32, (RANK, RANK), 1)
    eye = jnp.where(row == col, 1.0, 0.0).astype(F32)
    am[0] = g[...] * (1.0 / rows) + EPSILON * eye
    am[1] = eye
    sub = lax.broadcasted_iota(jnp.int32, (8, RANK), 0)
    for p in range(RANK // 8):
        lo = 8 * p
        blocks = RANK // 8 - p
        a = [am[0, lo + 8 * t : lo + 8 * t + 8, :] for t in range(blocks)]
        m = [am[1, lo + 8 * t : lo + 8 * t + 8, :] for t in range(blocks)]
        c = [
            [jnp.broadcast_to(a[t][:, lo + j : lo + j + 1], (8, RANK)) for t in range(blocks)]
            for j in range(8)
        ]
        diag = None
        for k in range(8):
            pivot = jnp.broadcast_to(c[k][0][k : k + 1, :], (8, RANK))
            diag = pivot if diag is None else jnp.where(sub == k, pivot, diag)
            recip = 1.0 / pivot
            mult = [c[k][t] * recip for t in range(blocks)]
            mult[0] = jnp.where(sub > k, mult[0], 0.0)
            for j in range(k + 1, 8):
                f = jnp.broadcast_to(c[j][0][k : k + 1, :], (8, RANK))
                for t in range(blocks):
                    c[j][t] = c[j][t] - mult[t] * f
            arow = jnp.broadcast_to(a[0][k : k + 1, :], (8, RANK))
            mrow = jnp.broadcast_to(m[0][k : k + 1, :], (8, RANK))
            for t in range(blocks):
                a[t] = a[t] - mult[t] * arow
                m[t] = m[t] - mult[t] * mrow
        am[1, lo : lo + 8, :] = m[0] * lax.rsqrt(diag)
        for t in range(1, blocks):
            am[0, lo + 8 * t : lo + 8 * t + 8, :] = a[t]
            am[1, lo + 8 * t : lo + 8 * t + 8, :] = m[t]
    w0, w1, w2 = split(am[1])
    near = jnp.concatenate([jnp.concatenate([w0, w1], 1), jnp.concatenate([w1, w0], 1)], 0)
    step = (BLOCKS * TB) // STEPS
    copies = []
    for s in range(STEPS):
        at = pl.ds(s * step, step)
        both = along(u[at, : 2 * RANK], near)
        tail = along(u[at, 2 * RANK :], w0) + along(u[at, :RANK], w2)
        o[at, :] = both[:, :RANK] + (both[:, RANK:] + tail)
        c = pltpu.make_async_copy(o.at[at], out_hbm.at[at], o_sem.at[s])
        c.start()
        copies.append(c)
    for c in copies:
        c.wait()


def finish(rows, g, u):
    n = BLOCKS * TB
    return pl.pallas_call(
        functools.partial(finish_kernel, rows),
        name="finish",
        out_shape=jax.ShapeDtypeStruct((n, RANK), F32),
        in_specs=[pl.BlockSpec(memory_space=pltpu.VMEM), pl.BlockSpec(memory_space=pltpu.VMEM)],
        out_specs=pl.BlockSpec(memory_space=pl.ANY),
        scratch_shapes=[
            pltpu.VMEM((n, RANK), F32),
            pltpu.VMEM((2, RANK, RANK), F32),
            pltpu.SemaphoreType.DMA((STEPS,)),
        ],
        compiler_params=pltpu.CompilerParams(vmem_limit_bytes=40 * 1024 * 1024),
    )(g, u)


def body(sketch, tile_values, sent_blocks, pair_counts):
    owners = lax.axis_size("shard")
    tiles = tile_values[0].reshape(PAIRS, EDGE, EDGE)
    u, g = exchange(owners, sent_blocks, pair_counts, sketch[0].reshape(BLOCKS, TB, RANK), tiles)
    rows = BLOCKS * TB * owners
    return finish(rows, g, u)[None]


def solution(mesh):
    return jax.shard_map(
        body,
        mesh=mesh,
        in_specs=(
            P("side", "shard", None),
            P("side", "shard", None),
            P(None, "shard"),
            P(None, "shard"),
        ),
        out_specs=P("side", "shard", None),
        check_vma=False,
    )
```

```python
import functools

import jax
import jax.numpy as jnp
from jax import lax
from jax.experimental import pallas as pl
from jax.experimental.pallas import tpu as pltpu
from jax.sharding import PartitionSpec as P

TB = 128
RANK = 128
PEER = 8
HALF = 2
PAIRS = 5
BLOCKS = 16
EDGE = PEER * TB
CHUNKS = 4
CROWS = EDGE // CHUNKS
RING = 4
PLANE = 16
PIECE = 32
CORNERS = (0, 3, 12, 15)
EARLY = (0, 1, 4, 2, 5, 8, 3, 6, 9, 12, 7, 10, 13, 11, 14, 15)
EPSILON = 1e-05
F32 = jnp.float32
BF16 = jnp.bfloat16
MESH = pl.DeviceIdType.MESH
HIGHEST = lax.Precision.HIGHEST


def split(x):
    high = x.astype(BF16)
    rest = x - high.astype(F32)
    middle = rest.astype(BF16)
    return high, middle, (rest - middle.astype(F32)).astype(BF16)


def gram(x):
    def cross(a, b):
        return lax.dot_general(a, b, (((0,), (0,)), ((), ())), preferred_element_type=F32)

    high, middle, low = split(x)
    pair = jnp.concatenate([high, middle], 1)
    both = cross(pair, pair)
    mixed = both[:RANK, RANK:] + cross(high, low)
    return both[:RANK, :RANK] + both[RANK:, RANK:] + mixed + mixed.T


def exchange_kernel(
    owners,
    lists_hbm,
    counts_hbm,
    sk_hbm,
    tile_hbm,
    u_parts,
    gsum,
    lists,
    counts,
    sk,
    tile,
    send,
    recv,
    relay,
    prod,
    u,
    inv,
    gpart,
    rs,
    ybuf,
    in_sem,
    tile_sem,
    a_send,
    a_recv,
    r_send,
    r_recv,
    b_send,
    b_recv,
    rs_send,
    rs_recv,
    y_send,
    y_recv,
    ag_send,
    ag_recv,
    plane_sem,
    hello_sem,
):
    side = lax.axis_index("side")
    me = lax.axis_index("shard")
    far = 1 - side
    ahead = lax.rem(me + 1, owners)
    behind = lax.rem(me + owners - 1, owners)
    planes = owners // PLANE
    q = lax.rem(me, PLANE)
    y = me // PLANE
    base = y * PLANE

    inputs = []
    for n, (src, dst) in enumerate(((sk_hbm, sk), (lists_hbm, lists), (counts_hbm, counts))):
        c = pltpu.make_async_copy(src, dst, in_sem.at[n])
        c.start()
        inputs.append(c)
    def signal(sem, device):
        pl.semaphore_signal(sem, inc=1, device_id=device, device_id_type=MESH)

    ring_z = [(side, me - lax.rem(me, RING) + lax.rem(me + i, RING)) for i in range(1, RING)]
    ring_x = [(side, base + lax.rem(q + i * RING, PLANE)) for i in range(1, RING)]
    ring_y = [(side, lax.rem(me + i * PLANE, owners)) for i in range(1, planes)]
    across = [(far, ahead), (far, behind), (far, me)]
    greet = [(side, ahead), (side, behind)] + ring_z + ring_x + ring_y
    barrier = pltpu.get_barrier_semaphore()
    for device in greet:
        signal(barrier, device)

    @pl.when(side == 0)
    def _():
        for device in across:
            signal(barrier, device)

    for c in inputs:
        c.wait()

    def pack(j):
        live = counts[side, j]
        for b in range(PEER):
            keep = jnp.where(b < live, 1.0, 0.0).astype(BF16)
            send[j, b * TB : (b + 1) * TB, :] = sk[lists[side, j * PEER + b]] * keep

    for j in (4, 0):
        pack(j)

    pl.semaphore_wait(barrier, len(greet) + side * len(across))
    for device in ring_x:
        signal(plane_sem, device)

    @pl.when(side == 1)
    def _():
        for device in across:
            signal(hello_sem, device)

    def remote(src, dst, ss, rsem, dev):
        c = pltpu.make_async_remote_copy(
            src_ref=src, dst_ref=dst, send_sem=ss, recv_sem=rsem, device_id=dev, device_id_type=MESH
        )
        return c

    rows = [pl.ds(i * CROWS, CROWS) for i in range(CHUNKS)]
    a_copies = [[], []]
    for i in range(CHUNKS):
        for way, (jj, to) in enumerate(((4, ahead), (0, behind))):
            c = remote(
                send.at[jj, rows[i]], relay.at[way, rows[i]], a_send.at[way, i], a_recv.at[way, i], (side, to)
            )
            c.start()
            a_copies[way].append(c)
    for j in (3, 1, 2):
        pack(j)

    @pl.when(side == 0)
    def _():
        pl.semaphore_wait(hello_sem, len(across))

    b_copies = {}
    for jj, to in ((2, me), (3, ahead), (1, behind)):
        c = remote(send.at[jj], recv.at[4 - jj], b_send.at[jj], b_recv.at[4 - jj], (far, to))
        c.start()
        b_copies[4 - jj] = c

    tile_copies = {}
    for j in (2, 1, 3, 0, 4):
        c = pltpu.make_async_copy(tile_hbm.at[j], tile.at[j], tile_sem.at[j])
        c.start()
        tile_copies[j] = c

    def table(n, carry):
        j = n // BLOCKS
        k = lax.rem(n, BLOCKS)
        place = jnp.int32(PEER)
        live = counts[side, j]
        for a in range(PEER):
            hit = jnp.logical_and(lists[side, j * PEER + a] == k, a < live)
            place = jnp.where(hit, jnp.int32(a), place)
        inv[n] = place
        return carry

    lax.fori_loop(0, PAIRS * BLOCKS, table, 0)
    for j in range(PAIRS):
        prod[j, PEER] = jnp.zeros((TB, RANK), F32)

    def multiply(j, k0, depth, first):
        def step(a, carry):
            at = pl.ds(pl.multiple_of(a * 2 * TB, 2 * TB), 2 * TB)
            part = jnp.dot(
                tile[j, at, k0 : k0 + depth], recv[j, k0 : k0 + depth, :], preferred_element_type=F32
            ).reshape(2, TB, RANK)
            where = pl.ds(a * 2, 2)
            if first:
                prod[j, where] = part
            else:
                prod[j, where] = prod[j, where] + part
            return carry

        lax.fori_loop(0, PEER // 2, step, 0)

    b_copies[2].wait_recv()
    tile_copies[2].wait()
    multiply(2, 0, EDGE, True)

    r_copies = [[], []]
    for i in range(CHUNKS):
        for way, (j, to) in enumerate(((0, ahead), (4, behind))):
            a_copies[way][i].wait_recv()
            c = remote(
                relay.at[way, rows[i]], recv.at[j, rows[i]], r_send.at[way, i], r_recv.at[way, i], (far, to)
            )
            c.start()
            r_copies[way].append(c)

    for j in (1, 3):
        b_copies[j].wait_recv()
        tile_copies[j].wait()
        multiply(j, 0, EDGE, True)

    def gather_near(k, carry):
        u[k] = (
            prod[1, inv[BLOCKS + k]] + prod[2, inv[2 * BLOCKS + k]] + prod[3, inv[3 * BLOCKS + k]]
        )
        return carry

    lax.fori_loop(0, BLOCKS, gather_near, 0)

    tile_copies[0].wait()
    tile_copies[4].wait()
    for i in range(CHUNKS):
        for way, j in enumerate((0, 4)):
            r_copies[way][i].wait_recv()
            part = jnp.dot(
                tile[j, :, i * CROWS : (i + 1) * CROWS], recv[j, rows[i], :], preferred_element_type=F32
            ).reshape(PEER, TB, RANK)
            if i == 0:
                prod[j, 0:PEER] = part
            else:
                prod[j, 0:PEER] = prod[j, 0:PEER] + part

    for k in range(BLOCKS):
        u[k] = u[k] + prod[0, inv[k]] + prod[4, inv[4 * BLOCKS + k]]
    gpart[...] = gram(u[...].reshape(BLOCKS * TB, RANK))

    pl.semaphore_wait(plane_sem, len(ring_x))
    def rs_copy(n, at):
        piece = gpart.at[pl.ds(n * PIECE, PIECE)]
        return remote(piece, rs.at[at], rs_send.at[n], rs_recv.at[at], (side, base + CORNERS[n]))

    for n, corner in enumerate(CORNERS):

        @pl.when(q != corner)
        def _(n=n):
            rs_copy(n, q).start()

    def part(k, carry):
        at = pl.ds(pl.multiple_of(k * TB, TB), TB)
        for n, piece in enumerate(split(u[k])):
            u_parts[at, n * RANK : (n + 1) * RANK] = piece
        return carry

    lax.fori_loop(0, BLOCKS, part, 0)

    x = q // RING
    z = lax.rem(q, RING)
    summing = jnp.logical_and(lax.rem(x, RING - 1) == 0, lax.rem(z, RING - 1) == 0)
    number = 2 * (x // (RING - 1)) + z // (RING - 1)
    mine = pl.ds(pl.multiple_of(number * PIECE, PIECE), PIECE)

    def y_copy(i):
        to = lax.rem(me + i * PLANE, owners)
        return remote(ybuf.at[y], ybuf.at[y], y_send.at[i], y_recv.at[y], (side, to))

    def ag_copy(to):
        return remote(gsum.at[mine], gsum.at[mine], ag_send.at[to], ag_recv.at[number], (side, base + to))

    @pl.when(summing)
    def _():
        total = gpart[mine, :]
        for i in range(1, PLANE):
            src = lax.rem(q + i, PLANE)
            remote(rs.at[src], rs.at[src], rs_send.at[0], rs_recv.at[src], (side, me)).wait_recv()
            total = total + rs[src]
        ybuf[y] = total
        for i in range(1, planes):
            y_copy(i).start()
        for i in range(1, planes):
            src = lax.rem(y + i, planes)
            remote(ybuf.at[src], ybuf.at[src], y_send.at[0], y_recv.at[src], (side, me)).wait_recv()
        total = ybuf[0]
        for i in range(1, planes):
            total = total + ybuf[i]
        gsum[mine, :] = total
        for to in EARLY:

            @pl.when(q != to)
            def _(to=to):
                ag_copy(to).start()

    for n, corner in enumerate(CORNERS):

        @pl.when(q != corner)
        def _(n=n):
            piece = gsum.at[pl.ds(n * PIECE, PIECE)]
            remote(piece, piece, ag_send.at[0], ag_recv.at[n], (side, me)).wait_recv()
            rs_copy(n, q).wait_send()

    @pl.when(summing)
    def _():
        for i in range(1, planes):
            y_copy(i).wait_send()
        for to in EARLY:

            @pl.when(q != to)
            def _(to=to):
                ag_copy(to).wait_send()

    for group in (a_copies[0], a_copies[1], r_copies[0], r_copies[1]):
        for c in group:
            c.wait_send()
    for c in b_copies.values():
        c.wait_send()


def exchange(owners, lists, counts, sketch, tiles):
    dma = pltpu.SemaphoreType.DMA
    vmem = pl.BlockSpec(memory_space=pltpu.VMEM)
    hbm = pl.BlockSpec(memory_space=pl.ANY)
    planes = owners // PLANE
    return pl.pallas_call(
        functools.partial(exchange_kernel, owners),
        name="exchange",
        out_shape=(
            pltpu.VMEM((BLOCKS * TB, 3 * RANK), BF16),
            pltpu.VMEM((RANK, RANK), F32),
        ),
        in_specs=[hbm, hbm, hbm, hbm],
        out_specs=(vmem, vmem),
        scratch_shapes=[
            pltpu.SMEM((2, PAIRS * PEER), jnp.int32),
            pltpu.SMEM((2, PAIRS), jnp.int32),
            pltpu.VMEM((BLOCKS, TB, RANK), BF16),
            pltpu.VMEM((PAIRS, EDGE, EDGE), BF16),
            pltpu.VMEM((PAIRS, EDGE, RANK), BF16),
            pltpu.VMEM((PAIRS, EDGE, RANK), BF16),
            pltpu.VMEM((2, EDGE, RANK), BF16),
            pltpu.VMEM((PAIRS, PEER + 1, TB, RANK), F32),
            pltpu.VMEM((BLOCKS, TB, RANK), F32),
            pltpu.SMEM((PAIRS * BLOCKS,), jnp.int32),
            pltpu.VMEM((RANK, RANK), F32),
            pltpu.VMEM((PLANE, PIECE, RANK), F32),
            pltpu.VMEM((planes, PIECE, RANK), F32),
            dma((3,)),
            dma((PAIRS,)),
            dma((2, CHUNKS)),
            dma((2, CHUNKS)),
            dma((2, CHUNKS)),
            dma((2, CHUNKS)),
            dma((PAIRS,)),
            dma((PAIRS,)),
            dma((PLANE,)),
            dma((PLANE,)),
            dma((planes,)),
            dma((planes,)),
            dma((PLANE,)),
            dma((PLANE,)),
            pltpu.SemaphoreType.REGULAR,
            pltpu.SemaphoreType.REGULAR,
        ],
        compiler_params=pltpu.CompilerParams(
            collective_id=0, has_side_effects=True, vmem_limit_bytes=40 * 1024 * 1024
        ),
    )(*[pltpu.with_memory_space_constraint(x, pltpu.HBM) for x in (lists, counts, sketch, tiles)])


STEPS = 4


def along(a, b):
    return lax.dot_general(a, b, (((1,), (1,)), ((), ())), preferred_element_type=F32)


def finish_kernel(rows, g, u, out_hbm, o, am, o_sem):
    row = lax.broadcasted_iota(jnp.int32, (RANK, RANK), 0)
    col = lax.broadcasted_iota(jnp.int32, (RANK, RANK), 1)
    eye = jnp.where(row == col, 1.0, 0.0).astype(F32)
    am[0] = g[...] * (1.0 / rows) + EPSILON * eye
    am[1] = eye
    sub = lax.broadcasted_iota(jnp.int32, (8, RANK), 0)
    for p in range(RANK // 8):
        lo = 8 * p
        blocks = RANK // 8 - p
        a = [am[0, lo + 8 * t : lo + 8 * t + 8, :] for t in range(blocks)]
        m = [am[1, lo + 8 * t : lo + 8 * t + 8, :] for t in range(blocks)]
        c = [
            [jnp.broadcast_to(a[t][:, lo + j : lo + j + 1], (8, RANK)) for t in range(blocks)]
            for j in range(8)
        ]
        diag = None
        for k in range(8):
            pivot = jnp.broadcast_to(c[k][0][k : k + 1, :], (8, RANK))
            diag = pivot if diag is None else jnp.where(sub == k, pivot, diag)
            recip = 1.0 / pivot
            mult = [c[k][t] * recip for t in range(blocks)]
            mult[0] = jnp.where(sub > k, mult[0], 0.0)
            for j in range(k + 1, 8):
                f = jnp.broadcast_to(c[j][0][k : k + 1, :], (8, RANK))
                for t in range(blocks):
                    c[j][t] = c[j][t] - mult[t] * f
            arow = jnp.broadcast_to(a[0][k : k + 1, :], (8, RANK))
            mrow = jnp.broadcast_to(m[0][k : k + 1, :], (8, RANK))
            for t in range(blocks):
                a[t] = a[t] - mult[t] * arow
                m[t] = m[t] - mult[t] * mrow
        am[1, lo : lo + 8, :] = m[0] * lax.rsqrt(diag)
        for t in range(1, blocks):
            am[0, lo + 8 * t : lo + 8 * t + 8, :] = a[t]
            am[1, lo + 8 * t : lo + 8 * t + 8, :] = m[t]
    w0, w1, w2 = split(am[1])
    near = jnp.concatenate([jnp.concatenate([w0, w1], 1), jnp.concatenate([w1, w0], 1)], 0)
    step = (BLOCKS * TB) // STEPS
    copies = []
    for s in range(STEPS):
        at = pl.ds(s * step, step)
        both = along(u[at, : 2 * RANK], near)
        tail = along(u[at, 2 * RANK :], w0) + along(u[at, :RANK], w2)
        o[at, :] = both[:, :RANK] + (both[:, RANK:] + tail)
        c = pltpu.make_async_copy(o.at[at], out_hbm.at[at], o_sem.at[s])
        c.start()
        copies.append(c)
    for c in copies:
        c.wait()


def finish(rows, g, u):
    n = BLOCKS * TB
    return pl.pallas_call(
        functools.partial(finish_kernel, rows),
        name="finish",
        out_shape=jax.ShapeDtypeStruct((n, RANK), F32),
        in_specs=[pl.BlockSpec(memory_space=pltpu.VMEM), pl.BlockSpec(memory_space=pltpu.VMEM)],
        out_specs=pl.BlockSpec(memory_space=pl.ANY),
        scratch_shapes=[
            pltpu.VMEM((n, RANK), F32),
            pltpu.VMEM((2, RANK, RANK), F32),
            pltpu.SemaphoreType.DMA((STEPS,)),
        ],
        compiler_params=pltpu.CompilerParams(vmem_limit_bytes=40 * 1024 * 1024),
    )(g, u)


def body(sketch, tile_values, sent_blocks, pair_counts):
    owners = lax.axis_size("shard")
    tiles = tile_values[0].reshape(PAIRS, EDGE, EDGE)
    u, g = exchange(owners, sent_blocks, pair_counts, sketch[0].reshape(BLOCKS, TB, RANK), tiles)
    rows = BLOCKS * TB * owners
    return finish(rows, g, u)[None]


def solution(mesh):
    return jax.shard_map(
        body,
        mesh=mesh,
        in_specs=(
            P("side", "shard", None),
            P("side", "shard", None),
            P(None, "shard"),
            P(None, "shard"),
        ),
        out_specs=P("side", "shard", None),
        check_vma=False,
    )
```

```python
import functools

import jax
import jax.numpy as jnp
from jax import lax
from jax.experimental import pallas as pl
from jax.experimental.pallas import tpu as pltpu
from jax.sharding import PartitionSpec as P

TB = 128
RANK = 128
PEER = 8
HALF = 2
PAIRS = 5
BLOCKS = 16
EDGE = PEER * TB
CHUNKS = 4
CROWS = EDGE // CHUNKS
RING = 4
PLANE = 16
PIECE = 32
CORNERS = (0, 3, 12, 15)
EARLY = (0, 1, 4, 2, 5, 8, 3, 6, 9, 12, 7, 10, 13, 11, 14, 15)
EPSILON = 1e-05
F32 = jnp.float32
BF16 = jnp.bfloat16
MESH = pl.DeviceIdType.MESH
HIGHEST = lax.Precision.HIGHEST


def split(x):
    high = x.astype(BF16)
    rest = x - high.astype(F32)
    middle = rest.astype(BF16)
    return high, middle, (rest - middle.astype(F32)).astype(BF16)


def gram(x):
    def cross(a, b):
        return lax.dot_general(a, b, (((0,), (0,)), ((), ())), preferred_element_type=F32)

    high, middle, low = split(x)
    pair = jnp.concatenate([high, middle], 1)
    both = cross(pair, pair)
    mixed = both[:RANK, RANK:] + cross(high, low)
    return both[:RANK, :RANK] + both[RANK:, RANK:] + mixed + mixed.T


def exchange_kernel(
    owners,
    lists_hbm,
    counts_hbm,
    sk_hbm,
    tile_hbm,
    u_parts,
    gsum,
    lists,
    counts,
    sk,
    tile,
    send,
    recv,
    relay,
    prod,
    u,
    inv,
    gpart,
    rs,
    ybuf,
    in_sem,
    tile_sem,
    a_send,
    a_recv,
    r_send,
    r_recv,
    b_send,
    b_recv,
    rs_send,
    rs_recv,
    y_send,
    y_recv,
    ag_send,
    ag_recv,
    plane_sem,
    hello_sem,
):
    side = lax.axis_index("side")
    me = lax.axis_index("shard")
    far = 1 - side
    ahead = lax.rem(me + 1, owners)
    behind = lax.rem(me + owners - 1, owners)
    planes = owners // PLANE
    q = lax.rem(me, PLANE)
    y = me // PLANE
    base = y * PLANE

    inputs = []
    for n, (src, dst) in enumerate(((sk_hbm, sk), (lists_hbm, lists), (counts_hbm, counts))):
        c = pltpu.make_async_copy(src, dst, in_sem.at[n])
        c.start()
        inputs.append(c)
    def signal(sem, device):
        pl.semaphore_signal(sem, inc=1, device_id=device, device_id_type=MESH)

    ring_z = [(side, me - lax.rem(me, RING) + lax.rem(me + i, RING)) for i in range(1, RING)]
    ring_x = [(side, base + lax.rem(q + i * RING, PLANE)) for i in range(1, RING)]
    ring_y = [(side, lax.rem(me + i * PLANE, owners)) for i in range(1, planes)]
    across = [(far, ahead), (far, behind), (far, me)]
    greet = [(side, ahead), (side, behind)] + ring_z + ring_x + ring_y
    barrier = pltpu.get_barrier_semaphore()
    for device in greet:
        signal(barrier, device)

    @pl.when(side == 0)
    def _():
        for device in across:
            signal(barrier, device)

    for c in inputs:
        c.wait()

    def pack(j):
        live = counts[side, j]
        for b in range(PEER):
            keep = jnp.where(b < live, 1.0, 0.0).astype(BF16)
            send[j, b * TB : (b + 1) * TB, :] = sk[lists[side, j * PEER + b]] * keep

    for j in (4, 0):
        pack(j)

    pl.semaphore_wait(barrier, len(greet) + side * len(across))
    for device in ring_x:
        signal(plane_sem, device)

    @pl.when(side == 1)
    def _():
        for device in across:
            signal(hello_sem, device)

    def remote(src, dst, ss, rsem, dev):
        c = pltpu.make_async_remote_copy(
            src_ref=src, dst_ref=dst, send_sem=ss, recv_sem=rsem, device_id=dev, device_id_type=MESH
        )
        return c

    rows = [pl.ds(i * CROWS, CROWS) for i in range(CHUNKS)]
    a_copies = [[], []]
    for i in range(CHUNKS):
        for way, (jj, to) in enumerate(((4, ahead), (0, behind))):
            c = remote(
                send.at[jj, rows[i]], relay.at[way, rows[i]], a_send.at[way, i], a_recv.at[way, i], (side, to)
            )
            c.start()
            a_copies[way].append(c)
    for j in (3, 1, 2):
        pack(j)

    @pl.when(side == 0)
    def _():
        pl.semaphore_wait(hello_sem, len(across))

    b_copies = {}
    for jj, to in ((2, me), (3, ahead), (1, behind)):
        c = remote(send.at[jj], recv.at[4 - jj], b_send.at[jj], b_recv.at[4 - jj], (far, to))
        c.start()
        b_copies[4 - jj] = c

    tile_copies = {}
    for j in (2, 1, 3, 0, 4):
        c = pltpu.make_async_copy(tile_hbm.at[j], tile.at[j], tile_sem.at[j])
        c.start()
        tile_copies[j] = c

    def table(n, carry):
        j = n // BLOCKS
        k = lax.rem(n, BLOCKS)
        place = jnp.int32(PEER)
        live = counts[side, j]
        for a in range(PEER):
            hit = jnp.logical_and(lists[side, j * PEER + a] == k, a < live)
            place = jnp.where(hit, jnp.int32(a), place)
        inv[n] = place
        return carry

    lax.fori_loop(0, PAIRS * BLOCKS, table, 0)
    for j in range(PAIRS):
        prod[j, PEER] = jnp.zeros((TB, RANK), F32)

    def multiply(j, k0, depth, first):
        def step(a, carry):
            at = pl.ds(pl.multiple_of(a * 2 * TB, 2 * TB), 2 * TB)
            part = jnp.dot(
                tile[j, at, k0 : k0 + depth], recv[j, k0 : k0 + depth, :], preferred_element_type=F32
            ).reshape(2, TB, RANK)
            where = pl.ds(a * 2, 2)
            if first:
                prod[j, where] = part
            else:
                prod[j, where] = prod[j, where] + part
            return carry

        lax.fori_loop(0, PEER // 2, step, 0)

    b_copies[2].wait_recv()
    tile_copies[2].wait()
    multiply(2, 0, EDGE, True)

    r_copies = [[], []]
    for i in range(CHUNKS):
        for way, (j, to) in enumerate(((0, ahead), (4, behind))):
            a_copies[way][i].wait_recv()
            c = remote(
                relay.at[way, rows[i]], recv.at[j, rows[i]], r_send.at[way, i], r_recv.at[way, i], (far, to)
            )
            c.start()
            r_copies[way].append(c)

    for j in (1, 3):
        b_copies[j].wait_recv()
        tile_copies[j].wait()
        multiply(j, 0, EDGE, True)

    def gather_near(k, carry):
        u[k] = (
            prod[1, inv[BLOCKS + k]] + prod[2, inv[2 * BLOCKS + k]] + prod[3, inv[3 * BLOCKS + k]]
        )
        return carry

    lax.fori_loop(0, BLOCKS, gather_near, 0)

    tile_copies[0].wait()
    tile_copies[4].wait()
    for i in range(CHUNKS):
        for way, j in enumerate((0, 4)):
            r_copies[way][i].wait_recv()
            part = jnp.dot(
                tile[j, :, i * CROWS : (i + 1) * CROWS], recv[j, rows[i], :], preferred_element_type=F32
            ).reshape(PEER, TB, RANK)
            if i == 0:
                prod[j, 0:PEER] = part
            else:
                prod[j, 0:PEER] = prod[j, 0:PEER] + part

    half = BLOCKS // 2
    sums = []
    for k0 in (0, half):
        for k in range(k0, k0 + half):
            u[k] = u[k] + prod[0, inv[k]] + prod[4, inv[4 * BLOCKS + k]]
        sums.append(gram(u[k0 : k0 + half].reshape(half * TB, RANK)))
    gpart[...] = sums[0] + sums[1]

    pl.semaphore_wait(plane_sem, len(ring_x))
    def rs_copy(n, at):
        piece = gpart.at[pl.ds(n * PIECE, PIECE)]
        return remote(piece, rs.at[at], rs_send.at[n], rs_recv.at[at], (side, base + CORNERS[n]))

    for n, corner in enumerate(CORNERS):

        @pl.when(q != corner)
        def _(n=n):
            rs_copy(n, q).start()

    def part(k, carry):
        at = pl.ds(pl.multiple_of(k * TB, TB), TB)
        for n, piece in enumerate(split(u[k])):
            u_parts[at, n * RANK : (n + 1) * RANK] = piece
        return carry

    lax.fori_loop(0, BLOCKS, part, 0)

    x = q // RING
    z = lax.rem(q, RING)
    summing = jnp.logical_and(lax.rem(x, RING - 1) == 0, lax.rem(z, RING - 1) == 0)
    number = 2 * (x // (RING - 1)) + z // (RING - 1)
    mine = pl.ds(pl.multiple_of(number * PIECE, PIECE), PIECE)

    def y_copy(i):
        to = lax.rem(me + i * PLANE, owners)
        return remote(ybuf.at[y], ybuf.at[y], y_send.at[i], y_recv.at[y], (side, to))

    def ag_copy(to):
        return remote(gsum.at[mine], gsum.at[mine], ag_send.at[to], ag_recv.at[number], (side, base + to))

    @pl.when(summing)
    def _():
        total = gpart[mine, :]
        for i in range(1, PLANE):
            src = lax.rem(q + i, PLANE)
            remote(rs.at[src], rs.at[src], rs_send.at[0], rs_recv.at[src], (side, me)).wait_recv()
            total = total + rs[src]
        ybuf[y] = total
        for i in range(1, planes):
            y_copy(i).start()
        for i in range(1, planes):
            src = lax.rem(y + i, planes)
            remote(ybuf.at[src], ybuf.at[src], y_send.at[0], y_recv.at[src], (side, me)).wait_recv()
        total = ybuf[0]
        for i in range(1, planes):
            total = total + ybuf[i]
        gsum[mine, :] = total
        for to in EARLY:

            @pl.when(q != to)
            def _(to=to):
                ag_copy(to).start()

    for n, corner in enumerate(CORNERS):

        @pl.when(q != corner)
        def _(n=n):
            piece = gsum.at[pl.ds(n * PIECE, PIECE)]
            remote(piece, piece, ag_send.at[0], ag_recv.at[n], (side, me)).wait_recv()
            rs_copy(n, q).wait_send()

    @pl.when(summing)
    def _():
        for i in range(1, planes):
            y_copy(i).wait_send()
        for to in EARLY:

            @pl.when(q != to)
            def _(to=to):
                ag_copy(to).wait_send()

    for group in (a_copies[0], a_copies[1], r_copies[0], r_copies[1]):
        for c in group:
            c.wait_send()
    for c in b_copies.values():
        c.wait_send()


def exchange(owners, lists, counts, sketch, tiles):
    dma = pltpu.SemaphoreType.DMA
    vmem = pl.BlockSpec(memory_space=pltpu.VMEM)
    hbm = pl.BlockSpec(memory_space=pl.ANY)
    planes = owners // PLANE
    return pl.pallas_call(
        functools.partial(exchange_kernel, owners),
        name="exchange",
        out_shape=(
            pltpu.VMEM((BLOCKS * TB, 3 * RANK), BF16),
            pltpu.VMEM((RANK, RANK), F32),
        ),
        in_specs=[hbm, hbm, hbm, hbm],
        out_specs=(vmem, vmem),
        scratch_shapes=[
            pltpu.SMEM((2, PAIRS * PEER), jnp.int32),
            pltpu.SMEM((2, PAIRS), jnp.int32),
            pltpu.VMEM((BLOCKS, TB, RANK), BF16),
            pltpu.VMEM((PAIRS, EDGE, EDGE), BF16),
            pltpu.VMEM((PAIRS, EDGE, RANK), BF16),
            pltpu.VMEM((PAIRS, EDGE, RANK), BF16),
            pltpu.VMEM((2, EDGE, RANK), BF16),
            pltpu.VMEM((PAIRS, PEER + 1, TB, RANK), F32),
            pltpu.VMEM((BLOCKS, TB, RANK), F32),
            pltpu.SMEM((PAIRS * BLOCKS,), jnp.int32),
            pltpu.VMEM((RANK, RANK), F32),
            pltpu.VMEM((PLANE, PIECE, RANK), F32),
            pltpu.VMEM((planes, PIECE, RANK), F32),
            dma((3,)),
            dma((PAIRS,)),
            dma((2, CHUNKS)),
            dma((2, CHUNKS)),
            dma((2, CHUNKS)),
            dma((2, CHUNKS)),
            dma((PAIRS,)),
            dma((PAIRS,)),
            dma((PLANE,)),
            dma((PLANE,)),
            dma((planes,)),
            dma((planes,)),
            dma((PLANE,)),
            dma((PLANE,)),
            pltpu.SemaphoreType.REGULAR,
            pltpu.SemaphoreType.REGULAR,
        ],
        compiler_params=pltpu.CompilerParams(
            collective_id=0, has_side_effects=True, vmem_limit_bytes=40 * 1024 * 1024
        ),
    )(*[pltpu.with_memory_space_constraint(x, pltpu.HBM) for x in (lists, counts, sketch, tiles)])


STEPS = 4


def along(a, b):
    return lax.dot_general(a, b, (((1,), (1,)), ((), ())), preferred_element_type=F32)


def spread(x, k):
    return jnp.broadcast_to(x[k : k + 1, :], (8, RANK))


def fill(x, k):
    return jnp.broadcast_to(x[:, k : k + 1], (8, RANK))


def finish_kernel(rows, g, u, out_hbm, o, am, o_sem):
    row = lax.broadcasted_iota(jnp.int32, (RANK, RANK), 0)
    col = lax.broadcasted_iota(jnp.int32, (RANK, RANK), 1)
    eye = jnp.where(row == col, 1.0, 0.0).astype(F32)
    am[0] = g[...] * (1.0 / rows) + EPSILON * eye
    am[1] = eye
    sub = lax.broadcasted_iota(jnp.int32, (8, RANK), 0)
    ahead = None
    for p in range(RANK // 8):
        lo = 8 * p
        blocks = RANK // 8 - p
        a = [am[0, lo + 8 * t : lo + 8 * t + 8, :] for t in range(blocks)]
        m = [am[1, lo + 8 * t : lo + 8 * t + 8, :] for t in range(blocks)]
        c = [[fill(a[t], lo + j) for t in range(blocks)] for j in range(8)]
        if ahead is not None:
            for j in range(8):
                c[j][0] = ahead[j]
        ahead = [fill(a[1], lo + 8 + j) for j in range(8)] if blocks > 1 else None
        diag = jnp.zeros((8, RANK), F32)
        for k in range(8):
            pivot = spread(c[k][0], k)
            diag = jnp.where(sub == k, pivot, diag)
            recip = 1.0 / pivot
            mult = [c[k][t] * recip for t in range(blocks)]
            mult[0] = jnp.where(sub > k, mult[0], 0.0)
            for j in range(k + 1, 8):
                f = spread(c[j][0], k)
                for t in range(blocks):
                    c[j][t] = c[j][t] - mult[t] * f
            if ahead is not None:
                for j in range(8):
                    ahead[j] = ahead[j] - mult[1] * spread(c[k][1], j)
            arow = spread(a[0], k)
            mrow = spread(m[0], k)
            for t in range(blocks):
                a[t] = a[t] - mult[t] * arow
                m[t] = m[t] - mult[t] * mrow
        am[1, lo : lo + 8, :] = m[0] * lax.rsqrt(diag)
        for t in range(1, blocks):
            am[0, lo + 8 * t : lo + 8 * t + 8, :] = a[t]
            am[1, lo + 8 * t : lo + 8 * t + 8, :] = m[t]
    w0, w1, w2 = split(am[1])
    near = jnp.concatenate([jnp.concatenate([w0, w1], 1), jnp.concatenate([w1, w0], 1)], 0)
    step = (BLOCKS * TB) // STEPS
    copies = []
    for s in range(STEPS):
        at = pl.ds(s * step, step)
        both = along(u[at, : 2 * RANK], near)
        tail = along(u[at, 2 * RANK :], w0) + along(u[at, :RANK], w2)
        o[at, :] = both[:, :RANK] + (both[:, RANK:] + tail)
        c = pltpu.make_async_copy(o.at[at], out_hbm.at[at], o_sem.at[s])
        c.start()
        copies.append(c)
    for c in copies:
        c.wait()


def finish(rows, g, u):
    n = BLOCKS * TB
    return pl.pallas_call(
        functools.partial(finish_kernel, rows),
        name="finish",
        out_shape=jax.ShapeDtypeStruct((n, RANK), F32),
        in_specs=[pl.BlockSpec(memory_space=pltpu.VMEM), pl.BlockSpec(memory_space=pltpu.VMEM)],
        out_specs=pl.BlockSpec(memory_space=pl.ANY),
        scratch_shapes=[
            pltpu.VMEM((n, RANK), F32),
            pltpu.VMEM((2, RANK, RANK), F32),
            pltpu.SemaphoreType.DMA((STEPS,)),
        ],
        compiler_params=pltpu.CompilerParams(vmem_limit_bytes=40 * 1024 * 1024),
    )(g, u)


def body(sketch, tile_values, sent_blocks, pair_counts):
    owners = lax.axis_size("shard")
    tiles = tile_values[0].reshape(PAIRS, EDGE, EDGE)
    u, g = exchange(owners, sent_blocks, pair_counts, sketch[0].reshape(BLOCKS, TB, RANK), tiles)
    rows = BLOCKS * TB * owners
    return finish(rows, g, u)[None]


def solution(mesh):
    return jax.shard_map(
        body,
        mesh=mesh,
        in_specs=(
            P("side", "shard", None),
            P("side", "shard", None),
            P(None, "shard"),
            P(None, "shard"),
        ),
        out_specs=P("side", "shard", None),
        check_vma=False,
    )
```

```python
import functools

import jax
import jax.numpy as jnp
from jax import lax
from jax.experimental import pallas as pl
from jax.experimental.pallas import tpu as pltpu
from jax.sharding import PartitionSpec as P

TB = 128
RANK = 128
PEER = 8
HALF = 2
PAIRS = 5
BLOCKS = 16
EDGE = PEER * TB
CHUNKS = 4
CROWS = EDGE // CHUNKS
RING = 4
PLANE = 16
PIECE = 32
CORNERS = (0, 3, 12, 15)
EARLY = (0, 1, 4, 2, 5, 8, 3, 6, 9, 12, 7, 10, 13, 11, 14, 15)
EPSILON = 1e-05
F32 = jnp.float32
BF16 = jnp.bfloat16
MESH = pl.DeviceIdType.MESH
HIGHEST = lax.Precision.HIGHEST


def split(x):
    high = x.astype(BF16)
    rest = x - high.astype(F32)
    middle = rest.astype(BF16)
    return high, middle, (rest - middle.astype(F32)).astype(BF16)


def gram(x):
    def cross(a, b):
        return lax.dot_general(a, b, (((0,), (0,)), ((), ())), preferred_element_type=F32)

    high, middle, low = split(x)
    pair = jnp.concatenate([high, middle], 1)
    both = cross(pair, pair)
    mixed = both[:RANK, RANK:] + cross(high, low)
    return both[:RANK, :RANK] + both[RANK:, RANK:] + mixed + mixed.T


def exchange_kernel(
    owners,
    lists_hbm,
    counts_hbm,
    sk_hbm,
    tile_hbm,
    u_parts,
    gsum,
    lists,
    counts,
    sk,
    tile,
    send,
    recv,
    relay,
    prod,
    u,
    inv,
    gpart,
    rs,
    ybuf,
    in_sem,
    tile_sem,
    a_send,
    a_recv,
    r_send,
    r_recv,
    b_send,
    b_recv,
    rs_send,
    rs_recv,
    y_send,
    y_recv,
    ag_send,
    ag_recv,
    plane_sem,
    hello_sem,
):
    side = lax.axis_index("side")
    me = lax.axis_index("shard")
    far = 1 - side
    ahead = lax.rem(me + 1, owners)
    behind = lax.rem(me + owners - 1, owners)
    planes = owners // PLANE
    q = lax.rem(me, PLANE)
    y = me // PLANE
    base = y * PLANE

    inputs = []
    for n, (src, dst) in enumerate(((sk_hbm, sk), (lists_hbm, lists), (counts_hbm, counts))):
        c = pltpu.make_async_copy(src, dst, in_sem.at[n])
        c.start()
        inputs.append(c)
    def signal(sem, device):
        pl.semaphore_signal(sem, inc=1, device_id=device, device_id_type=MESH)

    ring_z = [(side, me - lax.rem(me, RING) + lax.rem(me + i, RING)) for i in range(1, RING)]
    ring_x = [(side, base + lax.rem(q + i * RING, PLANE)) for i in range(1, RING)]
    ring_y = [(side, lax.rem(me + i * PLANE, owners)) for i in range(1, planes)]
    across = [(far, ahead), (far, behind), (far, me)]
    greet = [(side, ahead), (side, behind)] + ring_z + ring_x + ring_y
    barrier = pltpu.get_barrier_semaphore()
    for device in greet:
        signal(barrier, device)

    @pl.when(side == 0)
    def _():
        for device in across:
            signal(barrier, device)

    for c in inputs:
        c.wait()

    def pack(j):
        live = counts[side, j]
        for b in range(PEER):
            keep = jnp.where(b < live, 1.0, 0.0).astype(BF16)
            send[j, b * TB : (b + 1) * TB, :] = sk[lists[side, j * PEER + b]] * keep

    for j in (4, 0):
        pack(j)

    pl.semaphore_wait(barrier, len(greet) + side * len(across))
    for device in ring_x:
        signal(plane_sem, device)

    @pl.when(side == 1)
    def _():
        for device in across:
            signal(hello_sem, device)

    def remote(src, dst, ss, rsem, dev):
        c = pltpu.make_async_remote_copy(
            src_ref=src, dst_ref=dst, send_sem=ss, recv_sem=rsem, device_id=dev, device_id_type=MESH
        )
        return c

    rows = [pl.ds(i * CROWS, CROWS) for i in range(CHUNKS)]
    a_copies = [[], []]
    for i in range(CHUNKS):
        for way, (jj, to) in enumerate(((4, ahead), (0, behind))):
            c = remote(
                send.at[jj, rows[i]], relay.at[way, rows[i]], a_send.at[way, i], a_recv.at[way, i], (side, to)
            )
            c.start()
            a_copies[way].append(c)
    for j in (3, 1, 2):
        pack(j)

    @pl.when(side == 0)
    def _():
        pl.semaphore_wait(hello_sem, len(across))

    b_copies = {}
    for jj, to in ((2, me), (3, ahead), (1, behind)):
        c = remote(send.at[jj], recv.at[4 - jj], b_send.at[jj], b_recv.at[4 - jj], (far, to))
        c.start()
        b_copies[4 - jj] = c

    tile_copies = {}
    for j in (2, 1, 3, 0, 4):
        c = pltpu.make_async_copy(tile_hbm.at[j], tile.at[j], tile_sem.at[j])
        c.start()
        tile_copies[j] = c

    def table(n, carry):
        j = n // BLOCKS
        k = lax.rem(n, BLOCKS)
        place = jnp.int32(PEER)
        live = counts[side, j]
        for a in range(PEER):
            hit = jnp.logical_and(lists[side, j * PEER + a] == k, a < live)
            place = jnp.where(hit, jnp.int32(a), place)
        inv[n] = place
        return carry

    lax.fori_loop(0, PAIRS * BLOCKS, table, 0)
    for j in range(PAIRS):
        prod[j, PEER] = jnp.zeros((TB, RANK), F32)

    def multiply(j, k0, depth, first):
        def step(a, carry):
            at = pl.ds(pl.multiple_of(a * 2 * TB, 2 * TB), 2 * TB)
            part = jnp.dot(
                tile[j, at, k0 : k0 + depth], recv[j, k0 : k0 + depth, :], preferred_element_type=F32
            ).reshape(2, TB, RANK)
            where = pl.ds(a * 2, 2)
            if first:
                prod[j, where] = part
            else:
                prod[j, where] = prod[j, where] + part
            return carry

        lax.fori_loop(0, PEER // 2, step, 0)

    b_copies[2].wait_recv()
    tile_copies[2].wait()
    multiply(2, 0, EDGE, True)

    r_copies = [[], []]
    for i in range(CHUNKS):
        for way, (j, to) in enumerate(((0, ahead), (4, behind))):
            a_copies[way][i].wait_recv()
            c = remote(
                relay.at[way, rows[i]], recv.at[j, rows[i]], r_send.at[way, i], r_recv.at[way, i], (far, to)
            )
            c.start()
            r_copies[way].append(c)

    for j in (1, 3):
        b_copies[j].wait_recv()
        tile_copies[j].wait()
        multiply(j, 0, EDGE, True)

    def gather_near(k, carry):
        u[k] = (
            prod[1, inv[BLOCKS + k]] + prod[2, inv[2 * BLOCKS + k]] + prod[3, inv[3 * BLOCKS + k]]
        )
        return carry

    lax.fori_loop(0, BLOCKS, gather_near, 0)

    tile_copies[0].wait()
    tile_copies[4].wait()
    for i in range(CHUNKS):
        for way, j in enumerate((0, 4)):
            r_copies[way][i].wait_recv()
            part = jnp.dot(
                tile[j, :, i * CROWS : (i + 1) * CROWS], recv[j, rows[i], :], preferred_element_type=F32
            ).reshape(PEER, TB, RANK)
            if i == 0:
                prod[j, 0:PEER] = part
            else:
                prod[j, 0:PEER] = prod[j, 0:PEER] + part
            if i == CHUNKS - 1 and way == 0:
                for k in range(BLOCKS):
                    u[k] = u[k] + prod[0, inv[k]]

    half = BLOCKS // 2
    sums = []
    for k0 in (0, half):
        for k in range(k0, k0 + half):
            u[k] = u[k] + prod[4, inv[4 * BLOCKS + k]]
        sums.append(gram(u[k0 : k0 + half].reshape(half * TB, RANK)))
    gpart[...] = sums[0] + sums[1]

    pl.semaphore_wait(plane_sem, len(ring_x))
    def rs_copy(n, at):
        piece = gpart.at[pl.ds(n * PIECE, PIECE)]
        return remote(piece, rs.at[at], rs_send.at[n], rs_recv.at[at], (side, base + CORNERS[n]))

    for n, corner in enumerate(CORNERS):

        @pl.when(q != corner)
        def _(n=n):
            rs_copy(n, q).start()

    def part(k, carry):
        at = pl.ds(pl.multiple_of(k * TB, TB), TB)
        for n, piece in enumerate(split(u[k])):
            u_parts[at, n * RANK : (n + 1) * RANK] = piece
        return carry

    lax.fori_loop(0, BLOCKS, part, 0)

    x = q // RING
    z = lax.rem(q, RING)
    summing = jnp.logical_and(lax.rem(x, RING - 1) == 0, lax.rem(z, RING - 1) == 0)
    number = 2 * (x // (RING - 1)) + z // (RING - 1)
    mine = pl.ds(pl.multiple_of(number * PIECE, PIECE), PIECE)

    def y_copy(i):
        to = lax.rem(me + i * PLANE, owners)
        return remote(ybuf.at[y], ybuf.at[y], y_send.at[i], y_recv.at[y], (side, to))

    def ag_copy(to):
        return remote(gsum.at[mine], gsum.at[mine], ag_send.at[to], ag_recv.at[number], (side, base + to))

    @pl.when(summing)
    def _():
        total = gpart[mine, :]
        for i in range(1, PLANE):
            src = lax.rem(q + i, PLANE)
            remote(rs.at[src], rs.at[src], rs_send.at[0], rs_recv.at[src], (side, me)).wait_recv()
            total = total + rs[src]
        ybuf[y] = total
        for i in range(1, planes):
            y_copy(i).start()
        for i in range(1, planes):
            src = lax.rem(y + i, planes)
            remote(ybuf.at[src], ybuf.at[src], y_send.at[0], y_recv.at[src], (side, me)).wait_recv()
        total = ybuf[0]
        for i in range(1, planes):
            total = total + ybuf[i]
        gsum[mine, :] = total
        for to in EARLY:

            @pl.when(q != to)
            def _(to=to):
                ag_copy(to).start()

    for n, corner in enumerate(CORNERS):

        @pl.when(q != corner)
        def _(n=n):
            piece = gsum.at[pl.ds(n * PIECE, PIECE)]
            remote(piece, piece, ag_send.at[0], ag_recv.at[n], (side, me)).wait_recv()
            rs_copy(n, q).wait_send()

    @pl.when(summing)
    def _():
        for i in range(1, planes):
            y_copy(i).wait_send()
        for to in EARLY:

            @pl.when(q != to)
            def _(to=to):
                ag_copy(to).wait_send()

    for group in (a_copies[0], a_copies[1], r_copies[0], r_copies[1]):
        for c in group:
            c.wait_send()
    for c in b_copies.values():
        c.wait_send()


def exchange(owners, lists, counts, sketch, tiles):
    dma = pltpu.SemaphoreType.DMA
    vmem = pl.BlockSpec(memory_space=pltpu.VMEM)
    hbm = pl.BlockSpec(memory_space=pl.ANY)
    planes = owners // PLANE
    return pl.pallas_call(
        functools.partial(exchange_kernel, owners),
        name="exchange",
        out_shape=(
            pltpu.VMEM((BLOCKS * TB, 3 * RANK), BF16),
            pltpu.VMEM((RANK, RANK), F32),
        ),
        in_specs=[hbm, hbm, hbm, hbm],
        out_specs=(vmem, vmem),
        scratch_shapes=[
            pltpu.SMEM((2, PAIRS * PEER), jnp.int32),
            pltpu.SMEM((2, PAIRS), jnp.int32),
            pltpu.VMEM((BLOCKS, TB, RANK), BF16),
            pltpu.VMEM((PAIRS, EDGE, EDGE), BF16),
            pltpu.VMEM((PAIRS, EDGE, RANK), BF16),
            pltpu.VMEM((PAIRS, EDGE, RANK), BF16),
            pltpu.VMEM((2, EDGE, RANK), BF16),
            pltpu.VMEM((PAIRS, PEER + 1, TB, RANK), F32),
            pltpu.VMEM((BLOCKS, TB, RANK), F32),
            pltpu.SMEM((PAIRS * BLOCKS,), jnp.int32),
            pltpu.VMEM((RANK, RANK), F32),
            pltpu.VMEM((PLANE, PIECE, RANK), F32),
            pltpu.VMEM((planes, PIECE, RANK), F32),
            dma((3,)),
            dma((PAIRS,)),
            dma((2, CHUNKS)),
            dma((2, CHUNKS)),
            dma((2, CHUNKS)),
            dma((2, CHUNKS)),
            dma((PAIRS,)),
            dma((PAIRS,)),
            dma((PLANE,)),
            dma((PLANE,)),
            dma((planes,)),
            dma((planes,)),
            dma((PLANE,)),
            dma((PLANE,)),
            pltpu.SemaphoreType.REGULAR,
            pltpu.SemaphoreType.REGULAR,
        ],
        compiler_params=pltpu.CompilerParams(
            collective_id=0, has_side_effects=True, vmem_limit_bytes=40 * 1024 * 1024
        ),
    )(*[pltpu.with_memory_space_constraint(x, pltpu.HBM) for x in (lists, counts, sketch, tiles)])


STEPS = 4


def along(a, b):
    return lax.dot_general(a, b, (((1,), (1,)), ((), ())), preferred_element_type=F32)


def spread(x, k):
    return jnp.broadcast_to(x[k : k + 1, :], (8, RANK))


def fill(x, k):
    return jnp.broadcast_to(x[:, k : k + 1], (8, RANK))


def finish_kernel(rows, g, u, out_hbm, o, am, o_sem):
    row = lax.broadcasted_iota(jnp.int32, (RANK, RANK), 0)
    col = lax.broadcasted_iota(jnp.int32, (RANK, RANK), 1)
    eye = jnp.where(row == col, 1.0, 0.0).astype(F32)
    am[0] = g[...] * (1.0 / rows) + EPSILON * eye
    am[1] = eye
    sub = lax.broadcasted_iota(jnp.int32, (8, RANK), 0)
    ahead = None
    for p in range(RANK // 8):
        lo = 8 * p
        blocks = RANK // 8 - p
        a = [am[0, lo + 8 * t : lo + 8 * t + 8, :] for t in range(blocks)]
        m = [am[1, lo + 8 * t : lo + 8 * t + 8, :] for t in range(blocks)]
        c = [[fill(a[t], lo + j) for t in range(blocks)] for j in range(8)]
        if ahead is not None:
            for j in range(8):
                c[j][0] = ahead[j]
        ahead = [fill(a[1], lo + 8 + j) for j in range(8)] if blocks > 1 else None
        diag = jnp.zeros((8, RANK), F32)
        for k in range(8):
            pivot = spread(c[k][0], k)
            diag = jnp.where(sub == k, pivot, diag)
            recip = 1.0 / pivot
            mult = [c[k][t] * recip for t in range(blocks)]
            mult[0] = jnp.where(sub > k, mult[0], 0.0)
            for j in range(k + 1, 8):
                f = spread(c[j][0], k)
                for t in range(blocks):
                    c[j][t] = c[j][t] - mult[t] * f
            if ahead is not None:
                for j in range(8):
                    ahead[j] = ahead[j] - mult[1] * spread(c[k][1], j)
            arow = spread(a[0], k)
            mrow = spread(m[0], k)
            for t in range(blocks):
                a[t] = a[t] - mult[t] * arow
                m[t] = m[t] - mult[t] * mrow
        am[1, lo : lo + 8, :] = m[0] * lax.rsqrt(diag)
        for t in range(1, blocks):
            am[0, lo + 8 * t : lo + 8 * t + 8, :] = a[t]
            am[1, lo + 8 * t : lo + 8 * t + 8, :] = m[t]
    w0, w1, w2 = split(am[1])
    near = jnp.concatenate([jnp.concatenate([w0, w1], 1), jnp.concatenate([w1, w0], 1)], 0)
    step = (BLOCKS * TB) // STEPS
    copies = []
    for s in range(STEPS):
        at = pl.ds(s * step, step)
        both = along(u[at, : 2 * RANK], near)
        tail = along(u[at, 2 * RANK :], w0) + along(u[at, :RANK], w2)
        o[at, :] = both[:, :RANK] + (both[:, RANK:] + tail)
        c = pltpu.make_async_copy(o.at[at], out_hbm.at[at], o_sem.at[s])
        c.start()
        copies.append(c)
    for c in copies:
        c.wait()


def finish(rows, g, u):
    n = BLOCKS * TB
    return pl.pallas_call(
        functools.partial(finish_kernel, rows),
        name="finish",
        out_shape=jax.ShapeDtypeStruct((n, RANK), F32),
        in_specs=[pl.BlockSpec(memory_space=pltpu.VMEM), pl.BlockSpec(memory_space=pltpu.VMEM)],
        out_specs=pl.BlockSpec(memory_space=pl.ANY),
        scratch_shapes=[
            pltpu.VMEM((n, RANK), F32),
            pltpu.VMEM((2, RANK, RANK), F32),
            pltpu.SemaphoreType.DMA((STEPS,)),
        ],
        compiler_params=pltpu.CompilerParams(vmem_limit_bytes=40 * 1024 * 1024),
    )(g, u)


def body(sketch, tile_values, sent_blocks, pair_counts):
    owners = lax.axis_size("shard")
    tiles = tile_values[0].reshape(PAIRS, EDGE, EDGE)
    u, g = exchange(owners, sent_blocks, pair_counts, sketch[0].reshape(BLOCKS, TB, RANK), tiles)
    rows = BLOCKS * TB * owners
    return finish(rows, g, u)[None]


def solution(mesh):
    return jax.shard_map(
        body,
        mesh=mesh,
        in_specs=(
            P("side", "shard", None),
            P("side", "shard", None),
            P(None, "shard"),
            P(None, "shard"),
        ),
        out_specs=P("side", "shard", None),
        check_vma=False,
    )
```
